32 devices in a mesh: row: 8 (over z, y), col: 4 (over x, core).
Axes of the slice: x: 2, y: 2, z: 4, core: 2. Of those that a mesh axis runs over, the one named last changes fastest.
Arguments:
- three_centre: bfloat16 [192, 512, 512], P('row', 'col'), may hold values from -0.25 to 0.25
- tensor_pattern: int32 [192, 4, 4], P('row'), may hold values 0 or 1
- occ_density: bfloat16 [512, 512], P('row'), may hold values from -0.25 to 0.25
- virt_density: bfloat16 [512, 512], P('row'), may hold values from -0.25 to 0.25
- density_pattern: int32 [4, 4], replicated, may hold values 0 or 1
Outputs:
- response: float32 [192, 192], P('row')
The draws below stay inside these ranges and needn't reach their ends.
All inputs are finite; a program needn't handle non-finite values. No bound on the sum of `tensor_pattern` on one device may be relied on, other than what follows from the above.
Results may differ from the reference program's by a relative error of at most 0.0041.
Values may be sent and summed in bfloat16 or wider, within the bound.
A program may use at most 64 MiB of HBM per device.

```python
import jax
import jax.numpy as jnp
from jax import lax

BS = 128
NBLK = 4
NAO = 512
NAUX = 192


def with_ends(values, stream_key, smallest, largest):
    longest = values.shape.index(max(values.shape))
    spots = []
    for shift in (0, 1):
        where = [jax.random.randint(jax.random.fold_in(stream_key, axis), (), 0, length) for axis, length in enumerate(values.shape)]
        where[longest] = (where[longest] + shift) % values.shape[longest]
        spots.append(tuple(where))
    return values.at[spots[0]].set(smallest).at[spots[1]].set(largest)


def level_of(own_key, shape, shards, smallest, high):
    def one(dim, parts):
        draws = jax.random.uniform(jax.random.fold_in(jax.random.fold_in(own_key, 6), dim), (parts,), jnp.float32, smallest / len(shards), high / len(shards))
        return jnp.repeat(jnp.exp(draws), shape[dim] // parts).reshape((-1,) + (1,) * (len(shape) - dim - 1))

    factor_of = one(*shards[0])
    for cut in shards[1:]:
        factor_of = factor_of * one(*cut)
    return factor_of


def gaussian(rng, extent, width, reach, shards=(), kind=jnp.bfloat16):
    entries = jax.random.normal(rng, extent, jnp.float32) * width
    if len(shards) > 0:
        entries = level_of(rng, extent, shards, -0.22, 0.18) * entries
    return jnp.clip(entries, min=-reach, max=reach).astype(kind)


def setup_inputs(seed: int = 0) -> dict:
    arg_keys = jax.random.split(jax.random.key(seed), 6)
    return {
        "three_centre": gaussian(arg_keys[0], (NAUX, NAO, NAO), NAO ** -0.5, 0.25, ((0, 8), (1, 4))),
        "tensor_pattern": with_ends((jax.random.randint(arg_keys[1], (NAUX, NBLK, NBLK), 0, 4) < 3).astype(jnp.int32), jax.random.fold_in(arg_keys[1], 1), 0, 1),
        "occ_density": gaussian(arg_keys[2], (NAO, NAO), NAO ** -0.5, 0.25, ((0, 8),)),
        "virt_density": gaussian(arg_keys[3], (NAO, NAO), NAO ** -0.5, 0.25, ((0, 8),)),
        "density_pattern": with_ends((jax.random.randint(arg_keys[4], (NBLK, NBLK), 0, 4) < 3).astype(jnp.int32), jax.random.fold_in(arg_keys[4], 1), 0, 1),
    }


def expand_blocks(pattern, block_size, first, second):
    return jnp.repeat(jnp.repeat(pattern, block_size, first), block_size, second)


def reference(three_centre, tensor_pattern, occ_density, virt_density, density_pattern):
    density_mask = expand_blocks(density_pattern, BS, 0, 1).astype(occ_density.dtype)
    occupied = occ_density * density_mask
    virtual = virt_density * density_mask

    def per_aux(items):
        tensor_row, pattern_row = items
        masked = tensor_row * expand_blocks(pattern_row, BS, 0, 1).astype(tensor_row.dtype)
        moved = jnp.dot(masked, virtual, preferred_element_type=jnp.float32).astype(jnp.bfloat16)
        second = jnp.dot(occupied, moved, preferred_element_type=jnp.float32).astype(jnp.bfloat16)
        return second, masked

    second_all, masked_all = lax.map(per_aux, (three_centre, tensor_pattern))
    left_flat = second_all.reshape(NAUX, NAO * NAO)
    right_flat = masked_all.reshape(NAUX, NAO * NAO)
    return lax.dot_general(left_flat, right_flat, (((1,), (1,)), ((), ())), preferred_element_type=jnp.float32)
```

```python
import functools

import jax
import jax.numpy as jnp
from jax import lax
from jax.experimental import pallas as pl
from jax.experimental.pallas import tpu as pltpu
from jax.sharding import PartitionSpec as P

BS = 128
MESH = pl.DeviceIdType.MESH


def expand_blocks(pattern, block_size, first, second):
    return jnp.repeat(jnp.repeat(pattern, block_size, first), block_size, second)


def far_first(count):
    return sorted(range(1, count), key=lambda k: (abs(k - count / 2), k))


def greet(me_row, me_col, rows, cols):
    barrier = pltpu.get_barrier_semaphore()
    for i in range(rows):
        for j in range(cols):
            if i or j:
                pl.semaphore_signal(
                    barrier,
                    inc=1,
                    device_id=(lax.rem(me_row + i, rows), lax.rem(me_col + j, cols)),
                    device_id_type=MESH,
                )
    pl.semaphore_wait(barrier, rows * cols - 1)


def exchange_kernel(
    rows, cols,
    tensor_ref, pattern_ref, occ_ref, virt_ref, density_ref,
    b_out, s_out,
    masked, virt_all, occ_all, moved, moved_cols, second,
    gather_send, gather_recv, spread_send, spread_recv,
    b_send, b_recv, m_send, m_recv, s_send, s_recv, own_sem,
):
    me_row, me_col = lax.axis_index("row"), lax.axis_index("col")
    aux, local, orb = tensor_ref.shape
    strip = local // rows
    wide = orb // cols
    blocks = orb // BS
    quarter = virt_ref.shape[0] // cols
    row_steps = far_first(rows)

    def remote(src, dst, send, recv, to_row, to_col):
        copy = pltpu.make_async_remote_copy(
            src_ref=src, dst_ref=dst, send_sem=send, recv_sem=recv,
            device_id=(to_row, to_col), device_id_type=MESH,
        )
        copy.start()
        return copy

    greet(me_row, me_col, rows, cols)

    share = pl.ds(pl.multiple_of(me_col * quarter, quarter), quarter)
    gathers = []
    owns = []
    for d, (src, dst) in enumerate(((virt_ref, virt_all), (occ_ref, occ_all))):
        own = pltpu.make_async_copy(src.at[share], dst.at[me_row, me_col], own_sem.at[d])
        own.start()
        owns.append(own)
        gathers.append([
            remote(src.at[share], dst.at[me_row, me_col],
                   gather_send.at[d, k], gather_recv.at[d, k],
                   lax.rem(me_row + k, rows), me_col)
            for k in row_steps
        ])

    block_row = (me_col * local) // BS

    def mask_one(p, carry):
        for j in range(blocks):
            keep = pattern_ref[(p * blocks + block_row) * blocks + j].astype(jnp.float32)
            piece = tensor_ref[p, :, j * BS:(j + 1) * BS].astype(jnp.float32)
            masked[p, :, j * BS:(j + 1) * BS] = (piece * keep).astype(jnp.bfloat16)
        return carry

    lax.fori_loop(0, aux, mask_one, 0)

    b_copies = []
    for k in row_steps:
        to_row = lax.rem(me_row + k, rows)
        part = pl.ds(pl.multiple_of(to_row * strip, strip), strip)
        b_copies.append(remote(masked.at[:, part, :], b_out.at[me_row],
                               b_send.at[k], b_recv.at[k], to_row, me_col))
    own_part = pl.ds(pl.multiple_of(me_row * strip, strip), strip)
    own_b = pltpu.make_async_copy(masked.at[:, own_part, :], b_out.at[me_row], own_sem.at[2])
    own_b.start()

    spreads = []
    for d, full in enumerate((virt_all, occ_all)):
        owns[d].wait()
        for copy in gathers[d]:
            copy.wait_recv()
        spreads.append([
            remote(full.at[:, me_col], full.at[:, me_col],
                   spread_send.at[d, k], spread_recv.at[d, k],
                   me_row, lax.rem(me_col + k, cols))
            for k in range(1, cols)
        ])

    def take_density(full, d):
        for copy in spreads[d]:
            copy.wait()
        for copy in gathers[d]:
            copy.wait_send()
        values = full[...].reshape(orb, orb)
        lines = []
        for i in range(blocks):
            line = []
            for j in range(blocks):
                keep = density_ref[i * blocks + j].astype(jnp.float32)
                piece = values[i * BS:(i + 1) * BS, j * BS:(j + 1) * BS].astype(jnp.float32)
                line.append((piece * keep).astype(jnp.bfloat16))
            lines.append(jnp.concatenate(line, axis=1))
        full[...] = jnp.concatenate(lines, axis=0).reshape(full.shape)

    take_density(virt_all, 0)

    def move_one(p, carry):
        product = jnp.dot(masked[p], virt_all[...].reshape(orb, orb),
                          preferred_element_type=jnp.float32).astype(jnp.bfloat16)
        for j in range(cols):
            moved[j, p] = product[:, j * wide:(j + 1) * wide]
        return carry

    lax.fori_loop(0, aux, move_one, 0)

    m_copies = []
    for k in range(1, cols):
        to_col = lax.rem(me_col + k, cols)
        m_copies.append(remote(moved.at[to_col], moved_cols.at[me_col],
                               m_send.at[k], m_recv.at[k], me_row, to_col))
    own_m = pltpu.make_async_copy(moved.at[me_col], moved_cols.at[me_col], own_sem.at[3])
    own_m.start()

    take_density(occ_all, 1)
    own_m.wait()
    for copy in m_copies:
        copy.wait()

    def second_two(p, carry):
        rhs = jnp.concatenate(
            [moved_cols[:, 2 * p + h].reshape(orb, wide) for h in range(2)], axis=1)
        product = jnp.dot(occ_all[...].reshape(orb, orb), rhs,
                          preferred_element_type=jnp.float32).astype(jnp.bfloat16)
        for h in range(2):
            second[2 * p + h] = product[:, h * wide:(h + 1) * wide]
        return carry

    lax.fori_loop(0, aux // 2, second_two, 0)

    lanes = pl.ds(pl.multiple_of(me_col * wide, wide), wide)

    def strip_of(to_row, to_col):
        return pl.ds(pl.multiple_of(to_col * local + to_row * strip, strip), strip)

    s_copies = []
    for k in row_steps + [0]:
        for q in range(cols):
            if k or q:
                to_row, to_col = lax.rem(me_row + k, rows), lax.rem(me_col + q, cols)
                s_copies.append(remote(
                    second.at[:, strip_of(to_row, to_col), :],
                    s_out.at[me_row, :, :, lanes],
                    s_send.at[k, q], s_recv.at[k, q], to_row, to_col))
    own_s = pltpu.make_async_copy(second.at[:, strip_of(me_row, me_col), :],
                                  s_out.at[me_row, :, :, lanes], own_sem.at[4])
    own_s.start()

    own_b.wait()
    for copy in b_copies:
        copy.wait()
    own_s.wait()
    for copy in s_copies:
        copy.wait()


def sum_kernel(rows, cols, part_ref, out_ref, landed, total, others,
               row_send, row_recv, col_send, col_recv):
    me_row, me_col = lax.axis_index("row"), lax.axis_index("col")
    greet(me_row, me_col, rows, cols)
    copies = []
    for k in far_first(rows):
        to_row = lax.rem(me_row + k, rows)
        copy = pltpu.make_async_remote_copy(
            src_ref=part_ref.at[to_row], dst_ref=landed.at[k],
            send_sem=row_send.at[k], recv_sem=row_recv.at[k],
            device_id=(to_row, me_col), device_id_type=MESH)
        copy.start()
        copies.append(copy)
    for copy in copies:
        copy.wait()
    value = part_ref[me_row]
    for k in range(1, rows):
        value = value + landed[k]
    total[...] = value
    copies = []
    for k in range(1, cols):
        to_col = lax.rem(me_col + k, cols)
        copy = pltpu.make_async_remote_copy(
            src_ref=total, dst_ref=others.at[me_col],
            send_sem=col_send.at[k], recv_sem=col_recv.at[k],
            device_id=(me_row, to_col), device_id_type=MESH)
        copy.start()
        copies.append(copy)
    others[me_col] = total[...]
    for copy in copies:
        copy.wait()
    value = others[0]
    for k in range(1, cols):
        value = value + others[k]
    out_ref[...] = value


def direct(rows, cols, three_centre, tensor_pattern, occ_density, virt_density, density_pattern):
    aux, local, orb = three_centre.shape
    strip, wide = local // rows, orb // cols
    quarter = occ_density.shape[0] // cols
    bf16 = jnp.bfloat16
    dma = pltpu.SemaphoreType.DMA
    vmem = pl.BlockSpec(memory_space=pltpu.VMEM)
    smem = pl.BlockSpec(memory_space=pltpu.SMEM)
    landed = jax.ShapeDtypeStruct((rows, aux, strip, orb), bf16)
    b_all, s_all = pl.pallas_call(
        functools.partial(exchange_kernel, rows, cols),
        out_shape=(landed, landed),
        in_specs=[vmem, smem, vmem, vmem, smem],
        out_specs=(pl.BlockSpec(memory_space=pl.ANY),) * 2,
        scratch_shapes=[
            pltpu.VMEM((aux, local, orb), bf16),
            pltpu.VMEM((rows, cols, quarter, orb), bf16),
            pltpu.VMEM((rows, cols, quarter, orb), bf16),
            pltpu.VMEM((cols, aux, local, wide), bf16),
            pltpu.VMEM((cols, aux, local, wide), bf16),
            pltpu.VMEM((aux, orb, wide), bf16),
            dma((2, rows)), dma((2, rows)), dma((2, cols)), dma((2, cols)),
            dma((rows,)), dma((rows,)), dma((cols,)), dma((cols,)),
            dma((rows, cols)), dma((rows, cols)), dma((5,)),
        ],
        compiler_params=pltpu.CompilerParams(
            collective_id=0, has_side_effects=True, vmem_limit_bytes=40 * 2**20),
    )(three_centre, tensor_pattern.reshape(-1), occ_density, virt_density,
      density_pattern.reshape(-1))
    total = rows * aux
    partial_chi = lax.dot_general(
        s_all.reshape(total, strip, orb), b_all.reshape(total, strip, orb),
        (((1, 2), (1, 2)), ((), ())), preferred_element_type=jnp.float32)
    return pl.pallas_call(
        functools.partial(sum_kernel, rows, cols),
        out_shape=jax.ShapeDtypeStruct((aux, total), jnp.float32),
        in_specs=[vmem],
        out_specs=vmem,
        scratch_shapes=[
            pltpu.VMEM((rows, aux, total), jnp.float32),
            pltpu.VMEM((aux, total), jnp.float32),
            pltpu.VMEM((cols, aux, total), jnp.float32),
            dma((rows,)), dma((rows,)), dma((cols,)), dma((cols,)),
        ],
        compiler_params=pltpu.CompilerParams(collective_id=1, has_side_effects=True),
    )(partial_chi.reshape(rows, aux, total))


def staged(three_centre, tensor_pattern, occ_density, virt_density, density_pattern):
    aux_count = three_centre.shape[0]
    local_rows = three_centre.shape[1]
    orbital_count = three_centre.shape[2]
    offset = lax.axis_index("col") * local_rows
    row_blocks = (offset + jnp.arange(local_rows, dtype=jnp.int32)) // BS
    pattern_rows = jnp.take(tensor_pattern, row_blocks, axis=1)
    tensor_mask = jnp.repeat(pattern_rows, BS, 2).astype(jnp.bfloat16)
    masked = three_centre * tensor_mask
    occupied_full, virtual_full = (
        lax.all_gather(occ_density, "row", axis=0, tiled=True),
        lax.all_gather(virt_density, "row", axis=0, tiled=True),
    )
    density_mask = expand_blocks(density_pattern, BS, 0, 1).astype(jnp.bfloat16)
    occupied = occupied_full * density_mask
    virtual = virtual_full * density_mask
    moved = jnp.dot(
        masked.reshape(aux_count * local_rows, orbital_count),
        virtual,
        preferred_element_type=jnp.float32,
    ).astype(jnp.bfloat16)
    moved = moved.reshape(aux_count, local_rows, orbital_count)
    moved_cols, regrouped = (
        lax.all_to_all(moved, "col", split_axis=2, concat_axis=1, tiled=True),
        lax.all_to_all(masked, "col", split_axis=2, concat_axis=1, tiled=True),
    )
    second = jnp.einsum(
        "lm,pms->pls", occupied, moved_cols, preferred_element_type=jnp.float32
    ).astype(jnp.bfloat16)
    grouped_left, grouped_right = (
        lax.all_to_all(second, "row", split_axis=1, concat_axis=0, tiled=True),
        lax.all_to_all(regrouped, "row", split_axis=1, concat_axis=0, tiled=True),
    )
    total_aux = grouped_left.shape[0]
    left_flat = grouped_left.reshape(total_aux, -1)
    right_flat = grouped_right.reshape(total_aux, -1)
    partial_chi = lax.dot_general(
        left_flat, right_flat, (((1,), (1,)), ((), ())), preferred_element_type=jnp.float32
    )
    row_summed = lax.psum_scatter(partial_chi, "row", scatter_dimension=0, tiled=True)
    return lax.psum(row_summed, "col")


def solution(mesh):
    rows, cols = mesh.shape["row"], mesh.shape["col"]

    def per_device(three_centre, tensor_pattern, occ_density, virt_density, density_pattern):
        aux, local, orb = three_centre.shape
        aligned = (
            local % (16 * rows) == 0 and occ_density.shape[0] % (16 * cols) == 0
            and orb % (128 * cols) == 0 and BS % local == 0 and aux % 8 == 0
        )
        args = (three_centre, tensor_pattern, occ_density, virt_density, density_pattern)
        return direct(rows, cols, *args) if aligned else staged(*args)

    in_specs = (P("row", "col", None), P("row", None, None), P("row", None), P("row", None), P())
    out_specs = P("row", None)
    return jax.shard_map(
        per_device, mesh=mesh, in_specs=in_specs, out_specs=out_specs, check_vma=False
    )
```

```python
import functools

import jax
import jax.numpy as jnp
from jax import lax
from jax.experimental import pallas as pl
from jax.experimental.pallas import tpu as pltpu
from jax.sharding import PartitionSpec as P

BS = 128
MESH = pl.DeviceIdType.MESH


def expand_blocks(pattern, block_size, first, second):
    return jnp.repeat(jnp.repeat(pattern, block_size, first), block_size, second)


def partner(me, k, count):
    if count & (count - 1):
        return lax.rem(me + k, count), lax.rem(me + count - k, count)
    bit, other = 1, me
    while bit < count:
        if k & bit:
            other = other + bit - 2 * bit * ((me // bit) % 2)
        bit *= 2
    return other, other


def near_first(count):
    half = [k for k in range(2, count // 2)]
    return half + [1] * (count > 1) + [k for k in range(max(2, count // 2), count)]


def greet(me_row, me_col, rows, cols):
    barrier = pltpu.get_barrier_semaphore()
    for i in range(rows):
        for j in range(cols):
            if i or j:
                pl.semaphore_signal(
                    barrier,
                    inc=1,
                    device_id=(lax.rem(me_row + i, rows), lax.rem(me_col + j, cols)),
                    device_id_type=MESH,
                )
    pl.semaphore_wait(barrier, rows * cols - 1)


def exchange_kernel(
    rows, cols, chunks,
    tensor_ref, pattern_ref, occ_ref, virt_ref, density_ref,
    b_out, s_out,
    masked, virt_all, occ_all, moved, moved_cols, second,
    gather_send, gather_recv, spread_send, spread_recv,
    b_send, b_recv, m_send, m_recv, s_send, s_recv, own_sem, load_sem,
):
    me_row, me_col = lax.axis_index("row"), lax.axis_index("col")
    aux, local, orb = tensor_ref.shape
    strip = local // rows
    wide = orb // cols
    blocks = orb // BS
    quarter = virt_ref.shape[0] // cols
    row_steps = near_first(rows)

    def remote(src, dst, send, recv, to_row, to_col):
        copy = pltpu.make_async_remote_copy(
            src_ref=src, dst_ref=dst, send_sem=send, recv_sem=recv,
            device_id=(to_row, to_col), device_id_type=MESH,
        )
        copy.start()
        return copy

    load = pltpu.make_async_copy(tensor_ref, masked, load_sem)
    load.start()
    greet(me_row, me_col, rows, cols)

    share = pl.ds(pl.multiple_of(me_col * quarter, quarter), quarter)
    gathers = []
    owns = []
    for d, (src, dst) in enumerate(((virt_ref, virt_all), (occ_ref, occ_all))):
        own = pltpu.make_async_copy(src.at[share], dst.at[me_row, me_col], own_sem.at[d])
        own.start()
        owns.append(own)
        gathers.append([
            remote(src.at[share], dst.at[me_row, me_col],
                   gather_send.at[d, k], gather_recv.at[d, k],
                   partner(me_row, k, rows)[0], me_col)
            for k in row_steps
        ])

    block_row = (me_col * local) // BS

    def mask_one(p, carry):
        for j in range(blocks):
            keep = pattern_ref[block_row, j, p].astype(jnp.float32)
            piece = masked[p, :, j * BS:(j + 1) * BS].astype(jnp.float32)
            masked[p, :, j * BS:(j + 1) * BS] = (piece * keep).astype(jnp.bfloat16)
        return carry

    load.wait()
    lax.fori_loop(0, aux, mask_one, 0)

    b_copies = []
    for k in row_steps:
        to_row = partner(me_row, k, rows)[0]
        part = pl.ds(pl.multiple_of(to_row * strip, strip), strip)
        b_copies.append(remote(masked.at[:, part, :], b_out.at[me_row],
                               b_send.at[k], b_recv.at[k], to_row, me_col))
    own_part = pl.ds(pl.multiple_of(me_row * strip, strip), strip)
    own_b = pltpu.make_async_copy(masked.at[:, own_part, :], b_out.at[me_row], own_sem.at[2])
    own_b.start()

    spreads = []
    for d, full in enumerate((virt_all, occ_all)):
        owns[d].wait()
        for copy in gathers[d]:
            copy.wait_recv()
        spreads.append([
            remote(full.at[:, me_col], full.at[:, me_col],
                   spread_send.at[d, k], spread_recv.at[d, k],
                   me_row, partner(me_col, k, cols)[0])
            for k in range(1, cols)
        ])

    def take_density(full, d):
        for copy in spreads[d]:
            copy.wait()
        for copy in gathers[d]:
            copy.wait_send()
        values = full[...].reshape(orb, orb)
        lines = []
        for i in range(blocks):
            line = []
            for j in range(blocks):
                keep = density_ref[i, j].astype(jnp.float32)
                piece = values[i * BS:(i + 1) * BS, j * BS:(j + 1) * BS].astype(jnp.float32)
                line.append((piece * keep).astype(jnp.bfloat16))
            lines.append(jnp.concatenate(line, axis=1))
        full[...] = jnp.concatenate(lines, axis=0).reshape(full.shape)

    take_density(virt_all, 0)

    def move_one(p, carry):
        product = jnp.dot(masked[p], virt_all[...].reshape(orb, orb),
                          preferred_element_type=jnp.float32).astype(jnp.bfloat16)
        for j in range(cols):
            moved[j, p] = product[:, j * wide:(j + 1) * wide]
        return carry

    span = aux // chunks
    m_copies = []
    for h in range(chunks):
        lax.fori_loop(h * span, (h + 1) * span, move_one, 0)
        piece = pl.ds(h * span, span)
        copies = []
        for k in range(1, cols):
            to_col = partner(me_col, k, cols)[0]
            copies.append(remote(moved.at[to_col, piece], moved_cols.at[me_col, piece],
                                 m_send.at[h, k], m_recv.at[h, k], me_row, to_col))
        own = pltpu.make_async_copy(moved.at[me_col, piece], moved_cols.at[me_col, piece],
                                    own_sem.at[5 + h])
        own.start()
        m_copies.append(copies + [own])

    take_density(occ_all, 1)

    def second_two(p, carry):
        rhs = jnp.concatenate(
            [moved_cols[:, 2 * p + h].reshape(orb, wide) for h in range(2)], axis=1)
        product = jnp.dot(occ_all[...].reshape(orb, orb), rhs,
                          preferred_element_type=jnp.float32).astype(jnp.bfloat16)
        for h in range(2):
            second[2 * p + h] = product[:, h * wide:(h + 1) * wide]
        return carry

    lanes = pl.ds(pl.multiple_of(me_col * wide, wide), wide)

    def strip_of(to_row, to_col):
        return pl.ds(pl.multiple_of(to_col * local + to_row * strip, strip), strip)

    s_copies = []
    for h in range(chunks):
        piece = pl.ds(h * span, span)
        for copy in m_copies[h]:
            copy.wait()
        lax.fori_loop(h * span // 2, (h + 1) * span // 2, second_two, 0)
        for k in row_steps + [0]:
            for q in range(cols):
                if k or q:
                    to_row, to_col = partner(me_row, k, rows)[0], partner(me_col, q, cols)[0]
                    s_copies.append(remote(
                        second.at[piece, strip_of(to_row, to_col), :],
                        s_out.at[me_row, piece, :, lanes],
                        s_send.at[h, k, q], s_recv.at[h, k, q], to_row, to_col))
    own_s = pltpu.make_async_copy(second.at[:, strip_of(me_row, me_col), :],
                                  s_out.at[me_row, :, :, lanes], own_sem.at[4])
    own_s.start()

    own_b.wait()
    for copy in b_copies:
        copy.wait()
    own_s.wait()
    for copy in s_copies:
        copy.wait()


def sum_kernel(rows, cols, part_ref, out_ref, landed, total, others,
               row_send, row_recv, col_send, col_recv):
    me_row, me_col = lax.axis_index("row"), lax.axis_index("col")
    greet(me_row, me_col, rows, cols)
    copies = []
    for k in near_first(rows):
        to_row = partner(me_row, k, rows)[0]
        copy = pltpu.make_async_remote_copy(
            src_ref=part_ref.at[to_row], dst_ref=landed.at[k],
            send_sem=row_send.at[k], recv_sem=row_recv.at[k],
            device_id=(to_row, me_col), device_id_type=MESH)
        copy.start()
        copies.append(copy)
    for copy in copies:
        copy.wait()
    value = part_ref[me_row]
    for k in range(1, rows):
        value = value + landed[k]
    total[...] = value
    copies = []
    for k in range(1, cols):
        to_col = partner(me_col, k, cols)[0]
        copy = pltpu.make_async_remote_copy(
            src_ref=total, dst_ref=others.at[me_col],
            send_sem=col_send.at[k], recv_sem=col_recv.at[k],
            device_id=(me_row, to_col), device_id_type=MESH)
        copy.start()
        copies.append(copy)
    others[me_col] = total[...]
    for copy in copies:
        copy.wait()
    value = others[0]
    for k in range(1, cols):
        value = value + others[k]
    out_ref[...] = value


def direct(rows, cols, three_centre, tensor_pattern, occ_density, virt_density, density_pattern):
    aux, local, orb = three_centre.shape
    strip, wide = local // rows, orb // cols
    quarter = occ_density.shape[0] // cols
    bf16 = jnp.bfloat16
    chunks = max(n for n in (1, 2, 3, 4) if aux % (2 * n) == 0)
    dma = pltpu.SemaphoreType.DMA
    vmem = pl.BlockSpec(memory_space=pltpu.VMEM)
    smem = pl.BlockSpec(memory_space=pltpu.SMEM)
    hbm = pl.BlockSpec(memory_space=pltpu.MemorySpace.HBM)
    landed = jax.ShapeDtypeStruct((rows, aux, strip, orb), bf16)
    b_all, s_all = pl.pallas_call(
        functools.partial(exchange_kernel, rows, cols, chunks),
        out_shape=(landed, landed),
        in_specs=[hbm, smem, hbm, hbm, smem],
        out_specs=(pl.BlockSpec(memory_space=pl.ANY),) * 2,
        scratch_shapes=[
            pltpu.VMEM((aux, local, orb), bf16),
            pltpu.VMEM((rows, cols, quarter, orb), bf16),
            pltpu.VMEM((rows, cols, quarter, orb), bf16),
            pltpu.VMEM((cols, aux, local, wide), bf16),
            pltpu.VMEM((cols, aux, local, wide), bf16),
            pltpu.VMEM((aux, orb, wide), bf16),
            dma((2, rows)), dma((2, rows)), dma((2, cols)), dma((2, cols)),
            dma((rows,)), dma((rows,)), dma((chunks, cols)), dma((chunks, cols)),
            dma((chunks, rows, cols)), dma((chunks, rows, cols)), dma((5 + chunks,)), dma(()),
        ],
        compiler_params=pltpu.CompilerParams(
            collective_id=0, has_side_effects=True, vmem_limit_bytes=67_000_000),
    )(three_centre, tensor_pattern.transpose(1, 2, 0), occ_density, virt_density,
      density_pattern)
    total = rows * aux
    partial_chi = lax.dot_general(
        s_all.reshape(total, strip, orb), b_all.reshape(total, strip, orb),
        (((1, 2), (1, 2)), ((), ())), preferred_element_type=jnp.float32)
    return pl.pallas_call(
        functools.partial(sum_kernel, rows, cols),
        out_shape=jax.ShapeDtypeStruct((aux, total), jnp.float32),
        in_specs=[vmem],
        out_specs=vmem,
        scratch_shapes=[
            pltpu.VMEM((rows, aux, total), jnp.float32),
            pltpu.VMEM((aux, total), jnp.float32),
            pltpu.VMEM((cols, aux, total), jnp.float32),
            dma((rows,)), dma((rows,)), dma((cols,)), dma((cols,)),
        ],
        compiler_params=pltpu.CompilerParams(collective_id=1, has_side_effects=True),
    )(partial_chi.reshape(rows, aux, total))


def staged(three_centre, tensor_pattern, occ_density, virt_density, density_pattern):
    aux_count = three_centre.shape[0]
    local_rows = three_centre.shape[1]
    orbital_count = three_centre.shape[2]
    offset = lax.axis_index("col") * local_rows
    row_blocks = (offset + jnp.arange(local_rows, dtype=jnp.int32)) // BS
    pattern_rows = jnp.take(tensor_pattern, row_blocks, axis=1)
    tensor_mask = jnp.repeat(pattern_rows, BS, 2).astype(jnp.bfloat16)
    masked = three_centre * tensor_mask
    occupied_full, virtual_full = (
        lax.all_gather(occ_density, "row", axis=0, tiled=True),
        lax.all_gather(virt_density, "row", axis=0, tiled=True),
    )
    density_mask = expand_blocks(density_pattern, BS, 0, 1).astype(jnp.bfloat16)
    occupied = occupied_full * density_mask
    virtual = virtual_full * density_mask
    moved = jnp.dot(
        masked.reshape(aux_count * local_rows, orbital_count),
        virtual,
        preferred_element_type=jnp.float32,
    ).astype(jnp.bfloat16)
    moved = moved.reshape(aux_count, local_rows, orbital_count)
    moved_cols, regrouped = (
        lax.all_to_all(moved, "col", split_axis=2, concat_axis=1, tiled=True),
        lax.all_to_all(masked, "col", split_axis=2, concat_axis=1, tiled=True),
    )
    second = jnp.einsum(
        "lm,pms->pls", occupied, moved_cols, preferred_element_type=jnp.float32
    ).astype(jnp.bfloat16)
    grouped_left, grouped_right = (
        lax.all_to_all(second, "row", split_axis=1, concat_axis=0, tiled=True),
        lax.all_to_all(regrouped, "row", split_axis=1, concat_axis=0, tiled=True),
    )
    total_aux = grouped_left.shape[0]
    left_flat = grouped_left.reshape(total_aux, -1)
    right_flat = grouped_right.reshape(total_aux, -1)
    partial_chi = lax.dot_general(
        left_flat, right_flat, (((1,), (1,)), ((), ())), preferred_element_type=jnp.float32
    )
    row_summed = lax.psum_scatter(partial_chi, "row", scatter_dimension=0, tiled=True)
    return lax.psum(row_summed, "col")


def solution(mesh):
    rows, cols = mesh.shape["row"], mesh.shape["col"]

    def per_device(three_centre, tensor_pattern, occ_density, virt_density, density_pattern):
        aux, local, orb = three_centre.shape
        aligned = (
            local % (16 * rows) == 0 and occ_density.shape[0] % (16 * cols) == 0
            and orb % (128 * cols) == 0 and BS % local == 0 and aux % 8 == 0
        )
        args = (three_centre, tensor_pattern, occ_density, virt_density, density_pattern)
        return direct(rows, cols, *args) if aligned else staged(*args)

    in_specs = (P("row", "col", None), P("row", None, None), P("row", None), P("row", None), P())
    out_specs = P("row", None)
    return jax.shard_map(
        per_device, mesh=mesh, in_specs=in_specs, out_specs=out_specs, check_vma=False
    )
```

```python
import functools

import jax
import jax.numpy as jnp
from jax import lax
from jax.experimental import pallas as pl
from jax.experimental.pallas import tpu as pltpu
from jax.sharding import PartitionSpec as P

BS = 128
MESH = pl.DeviceIdType.MESH


def expand_blocks(pattern, block_size, first, second):
    return jnp.repeat(jnp.repeat(pattern, block_size, first), block_size, second)


def partner(me, k, count):
    if count & (count - 1):
        return lax.rem(me + k, count), lax.rem(me + count - k, count)
    bit, other = 1, me
    while bit < count:
        if k & bit:
            other = other + bit - 2 * bit * ((me // bit) % 2)
        bit *= 2
    return other, other


def near_first(count):
    half = [k for k in range(2, count // 2)]
    return half + [1] * (count > 1) + [k for k in range(max(2, count // 2), count)]


def greet(me_row, me_col, rows, cols):
    barrier = pltpu.get_barrier_semaphore()
    for i in range(rows):
        for j in range(cols):
            if i or j:
                pl.semaphore_signal(
                    barrier,
                    inc=1,
                    device_id=(lax.rem(me_row + i, rows), lax.rem(me_col + j, cols)),
                    device_id_type=MESH,
                )
    pl.semaphore_wait(barrier, rows * cols - 1)


def exchange_kernel(
    rows, cols, chunks,
    tensor_ref, pattern_ref, occ_ref, virt_ref, density_ref,
    out_ref,
    b_in, s_in, b_lines, wide_rows, part, landed, total, others,
    masked, virt_all, occ_all, moved, moved_cols, second,
    gather_send, gather_recv, spread_send, spread_recv,
    b_send, b_recv, m_send, m_recv, s_send, s_recv, own_sem, load_sem, row_send, row_recv, col_send, col_recv,
):
    me_row, me_col = lax.axis_index("row"), lax.axis_index("col")
    aux, local, orb = tensor_ref.shape
    strip = local // rows
    wide = orb // cols
    blocks = orb // BS
    quarter = virt_ref.shape[0] // cols
    row_steps = near_first(rows)

    def remote(src, dst, send, recv, to_row, to_col):
        copy = pltpu.make_async_remote_copy(
            src_ref=src, dst_ref=dst, send_sem=send, recv_sem=recv,
            device_id=(to_row, to_col), device_id_type=MESH,
        )
        copy.start()
        return copy

    load = pltpu.make_async_copy(tensor_ref, masked, load_sem)
    load.start()
    greet(me_row, me_col, rows, cols)

    share = pl.ds(pl.multiple_of(me_col * quarter, quarter), quarter)
    gathers = []
    owns = []
    for d, (src, dst) in enumerate(((virt_ref, virt_all), (occ_ref, occ_all))):
        own = pltpu.make_async_copy(src.at[share], dst.at[me_row, me_col], own_sem.at[d])
        own.start()
        owns.append(own)
        gathers.append([
            remote(src.at[share], dst.at[me_row, me_col],
                   gather_send.at[d, k], gather_recv.at[d, k],
                   partner(me_row, k, rows)[0], me_col)
            for k in row_steps
        ])

    block_row = (me_col * local) // BS

    def mask_one(p, carry):
        for j in range(blocks):
            keep = pattern_ref[block_row, j, p].astype(jnp.float32)
            piece = masked[p, :, j * BS:(j + 1) * BS].astype(jnp.float32)
            masked[p, :, j * BS:(j + 1) * BS] = (piece * keep).astype(jnp.bfloat16)
        return carry

    load.wait()
    lax.fori_loop(0, aux, mask_one, 0)

    b_copies = []
    for k in row_steps:
        to_row = partner(me_row, k, rows)[0]
        theirs = pl.ds(pl.multiple_of(to_row * strip, strip), strip)
        b_copies.append(remote(masked.at[:, theirs, :], b_in.at[me_row],
                               b_send.at[k], b_recv.at[k], to_row, me_col))
    own_part = pl.ds(pl.multiple_of(me_row * strip, strip), strip)
    own_b = pltpu.make_async_copy(masked.at[:, own_part, :], b_in.at[me_row], own_sem.at[2])
    own_b.start()

    spreads = []
    for d, full in enumerate((virt_all, occ_all)):
        owns[d].wait()
        for copy in gathers[d]:
            copy.wait_recv()
        spreads.append([
            remote(full.at[:, me_col], full.at[:, me_col],
                   spread_send.at[d, k], spread_recv.at[d, k],
                   me_row, partner(me_col, k, cols)[0])
            for k in range(1, cols)
        ])

    def take_density(full, d):
        for copy in spreads[d]:
            copy.wait()
        for copy in gathers[d]:
            copy.wait_send()
        values = full[...].reshape(orb, orb)
        lines = []
        for i in range(blocks):
            line = []
            for j in range(blocks):
                keep = density_ref[i, j].astype(jnp.float32)
                piece = values[i * BS:(i + 1) * BS, j * BS:(j + 1) * BS].astype(jnp.float32)
                line.append((piece * keep).astype(jnp.bfloat16))
            lines.append(jnp.concatenate(line, axis=1))
        full[...] = jnp.concatenate(lines, axis=0).reshape(full.shape)

    take_density(virt_all, 0)

    def move_one(p, carry):
        product = jnp.dot(masked[p], virt_all[...].reshape(orb, orb),
                          preferred_element_type=jnp.float32).astype(jnp.bfloat16)
        for j in range(cols):
            moved[j, p] = product[:, j * wide:(j + 1) * wide]
        return carry

    span = aux // chunks
    m_copies = []
    for h in range(chunks):
        lax.fori_loop(h * span, (h + 1) * span, move_one, 0)
        piece = pl.ds(h * span, span)
        copies = []
        for k in range(1, cols):
            to_col = partner(me_col, k, cols)[0]
            copies.append(remote(moved.at[to_col, piece], moved_cols.at[me_col, piece],
                                 m_send.at[h, k], m_recv.at[h, k], me_row, to_col))
        own = pltpu.make_async_copy(moved.at[me_col, piece], moved_cols.at[me_col, piece],
                                    own_sem.at[5 + h])
        own.start()
        m_copies.append(copies + [own])

    take_density(occ_all, 1)

    def second_two(p, carry):
        rhs = jnp.concatenate(
            [moved_cols[:, 2 * p + h].reshape(orb, wide) for h in range(2)], axis=1)
        product = jnp.dot(occ_all[...].reshape(orb, orb), rhs,
                          preferred_element_type=jnp.float32).astype(jnp.bfloat16)
        for h in range(2):
            second[2 * p + h] = product[:, h * wide:(h + 1) * wide]
        return carry

    lanes = pl.ds(pl.multiple_of(me_col * wide, wide), wide)

    def strip_of(to_row, to_col):
        return pl.ds(pl.multiple_of(to_col * local + to_row * strip, strip), strip)

    s_copies = [[] for _ in range(chunks)]
    for h in range(chunks):
        piece = pl.ds(h * span, span)
        for copy in m_copies[h]:
            copy.wait()
        lax.fori_loop(h * span // 2, (h + 1) * span // 2, second_two, 0)
        for k in row_steps + [0]:
            for q in range(cols):
                if k or q:
                    to_row, to_col = partner(me_row, k, rows)[0], partner(me_col, q, cols)[0]
                    s_copies[h].append(remote(
                        second.at[piece, strip_of(to_row, to_col), :],
                        s_in.at[me_row, piece, :, lanes],
                        s_send.at[h, k, q], s_recv.at[h, k, q], to_row, to_col))
    own_s = pltpu.make_async_copy(second.at[:, strip_of(me_row, me_col), :],
                                  s_in.at[me_row, :, :, lanes], own_sem.at[4])
    own_s.start()

    def widen(p, carry):
        rows_at = pl.ds(pl.multiple_of(p * aux * strip, aux * strip), aux * strip)
        for j in range(orb // BS):
            wide_rows[j, rows_at, :] = b_in[p, :, :, j * BS:(j + 1) * BS].reshape(
                aux * strip, BS).astype(jnp.float32)
        return carry

    def every(line, count):
        return jnp.concatenate(
            [wide_rows[j, pl.ds(line, count, stride=strip), :] for j in range(orb // BS)],
            axis=1).astype(jnp.bfloat16)

    own_b.wait()
    for copy in b_copies:
        copy.wait()
    lax.fori_loop(0, rows, widen, 0)
    for line in range(strip):
        b_lines[line] = every(line, rows * aux)

    own_s.wait()
    for h in range(chunks):
        for copy in s_copies[h]:
            copy.wait()
        count = rows * span
        for j in range(orb // BS):
            wide_rows[j, 0:count * strip, :] = s_in[
                :, h * span:(h + 1) * span, :, j * BS:(j + 1) * BS].reshape(
                count * strip, BS).astype(jnp.float32)
        chi = jnp.zeros((count, rows * aux), jnp.float32)
        for line in range(strip):
            chi = chi + lax.dot_general(every(line, count), b_lines[line], (((1,), (1,)), ((), ())),
                                        preferred_element_type=jnp.float32)
        part[:, h * span:(h + 1) * span, :] = chi.reshape(rows, span, rows * aux)

    copies = []
    for k in row_steps:
        to_row = partner(me_row, k, rows)[0]
        copies.append(remote(part.at[to_row], landed.at[k],
                             row_send.at[k], row_recv.at[k], to_row, me_col))
    value = part[me_row]
    for copy in copies:
        copy.wait()
    for k in range(1, rows):
        value = value + landed[k]
    total[...] = value
    copies = []
    for k in range(1, cols):
        to_col = partner(me_col, k, cols)[0]
        copies.append(remote(total, others.at[me_col],
                             col_send.at[k], col_recv.at[k], me_row, to_col))
    others[me_col] = value
    for copy in copies:
        copy.wait()
    value = others[0]
    for k in range(1, cols):
        value = value + others[k]
    out_ref[...] = value


def direct(rows, cols, three_centre, tensor_pattern, occ_density, virt_density, density_pattern):
    aux, local, orb = three_centre.shape
    strip, wide = local // rows, orb // cols
    quarter = occ_density.shape[0] // cols
    bf16 = jnp.bfloat16
    chunks = aux // 8
    total = rows * aux
    f32 = jnp.float32
    dma = pltpu.SemaphoreType.DMA
    vmem = pl.BlockSpec(memory_space=pltpu.VMEM)
    smem = pl.BlockSpec(memory_space=pltpu.SMEM)
    hbm = pl.BlockSpec(memory_space=pltpu.MemorySpace.HBM)
    return pl.pallas_call(
        functools.partial(exchange_kernel, rows, cols, chunks),
        out_shape=jax.ShapeDtypeStruct((aux, total), f32),
        in_specs=[hbm, smem, hbm, hbm, smem],
        out_specs=vmem,
        scratch_shapes=[
            pltpu.VMEM((rows, aux, strip, orb), bf16),
            pltpu.VMEM((rows, aux, strip, orb), bf16),
            pltpu.VMEM((strip, total, orb), bf16),
            pltpu.VMEM((orb // BS, total * strip, BS), f32),
            pltpu.VMEM((rows, aux, total), f32),
            pltpu.VMEM((rows, aux, total), f32),
            pltpu.VMEM((aux, total), f32),
            pltpu.VMEM((cols, aux, total), f32),
            pltpu.VMEM((aux, local, orb), bf16),
            pltpu.VMEM((rows, cols, quarter, orb), bf16),
            pltpu.VMEM((rows, cols, quarter, orb), bf16),
            pltpu.VMEM((cols, aux, local, wide), bf16),
            pltpu.VMEM((cols, aux, local, wide), bf16),
            pltpu.VMEM((aux, orb, wide), bf16),
            dma((2, rows)), dma((2, rows)), dma((2, cols)), dma((2, cols)),
            dma((rows,)), dma((rows,)), dma((chunks, cols)), dma((chunks, cols)),
            dma((chunks, rows, cols)), dma((chunks, rows, cols)), dma((5 + chunks,)), dma(()),
            dma((rows,)), dma((rows,)), dma((cols,)), dma((cols,)),
        ],
        compiler_params=pltpu.CompilerParams(
            collective_id=0, has_side_effects=True, vmem_limit_bytes=67_000_000),
    )(three_centre, tensor_pattern.transpose(1, 2, 0), occ_density, virt_density,
      density_pattern)


def staged(three_centre, tensor_pattern, occ_density, virt_density, density_pattern):
    aux_count = three_centre.shape[0]
    local_rows = three_centre.shape[1]
    orbital_count = three_centre.shape[2]
    offset = lax.axis_index("col") * local_rows
    row_blocks = (offset + jnp.arange(local_rows, dtype=jnp.int32)) // BS
    pattern_rows = jnp.take(tensor_pattern, row_blocks, axis=1)
    tensor_mask = jnp.repeat(pattern_rows, BS, 2).astype(jnp.bfloat16)
    masked = three_centre * tensor_mask
    occupied_full, virtual_full = (
        lax.all_gather(occ_density, "row", axis=0, tiled=True),
        lax.all_gather(virt_density, "row", axis=0, tiled=True),
    )
    density_mask = expand_blocks(density_pattern, BS, 0, 1).astype(jnp.bfloat16)
    occupied = occupied_full * density_mask
    virtual = virtual_full * density_mask
    moved = jnp.dot(
        masked.reshape(aux_count * local_rows, orbital_count),
        virtual,
        preferred_element_type=jnp.float32,
    ).astype(jnp.bfloat16)
    moved = moved.reshape(aux_count, local_rows, orbital_count)
    moved_cols, regrouped = (
        lax.all_to_all(moved, "col", split_axis=2, concat_axis=1, tiled=True),
        lax.all_to_all(masked, "col", split_axis=2, concat_axis=1, tiled=True),
    )
    second = jnp.einsum(
        "lm,pms->pls", occupied, moved_cols, preferred_element_type=jnp.float32
    ).astype(jnp.bfloat16)
    grouped_left, grouped_right = (
        lax.all_to_all(second, "row", split_axis=1, concat_axis=0, tiled=True),
        lax.all_to_all(regrouped, "row", split_axis=1, concat_axis=0, tiled=True),
    )
    total_aux = grouped_left.shape[0]
    left_flat = grouped_left.reshape(total_aux, -1)
    right_flat = grouped_right.reshape(total_aux, -1)
    partial_chi = lax.dot_general(
        left_flat, right_flat, (((1,), (1,)), ((), ())), preferred_element_type=jnp.float32
    )
    row_summed = lax.psum_scatter(partial_chi, "row", scatter_dimension=0, tiled=True)
    return lax.psum(row_summed, "col")


def solution(mesh):
    rows, cols = mesh.shape["row"], mesh.shape["col"]

    def per_device(three_centre, tensor_pattern, occ_density, virt_density, density_pattern):
        aux, local, orb = three_centre.shape
        aligned = (
            local % (16 * rows) == 0 and occ_density.shape[0] % (16 * cols) == 0
            and orb % (128 * cols) == 0 and BS % local == 0 and aux % 8 == 0
        )
        args = (three_centre, tensor_pattern, occ_density, virt_density, density_pattern)
        return direct(rows, cols, *args) if aligned else staged(*args)

    in_specs = (P("row", "col", None), P("row", None, None), P("row", None), P("row", None), P())
    out_specs = P("row", None)
    return jax.shard_map(
        per_device, mesh=mesh, in_specs=in_specs, out_specs=out_specs, check_vma=False
    )
```

```python
import functools

import jax
import jax.numpy as jnp
from jax import lax
from jax.experimental import pallas as pl
from jax.experimental.pallas import tpu as pltpu
from jax.sharding import PartitionSpec as P

BS = 128
MESH = pl.DeviceIdType.MESH


def expand_blocks(pattern, block_size, first, second):
    return jnp.repeat(jnp.repeat(pattern, block_size, first), block_size, second)


def partner(me, k, count):
    if count & (count - 1):
        return lax.rem(me + k, count), lax.rem(me + count - k, count)
    bit, other = 1, me
    while bit < count:
        if k & bit:
            other = other + bit - 2 * bit * ((me // bit) % 2)
        bit *= 2
    return other, other


def near_first(count):
    half = [k for k in range(2, count // 2)]
    return half + [1] * (count > 1) + [k for k in range(max(2, count // 2), count)]


def greet(me_row, me_col, rows, cols):
    barrier = pltpu.get_barrier_semaphore()
    for i in range(rows):
        for j in range(cols):
            if i or j:
                pl.semaphore_signal(
                    barrier,
                    inc=1,
                    device_id=(lax.rem(me_row + i, rows), lax.rem(me_col + j, cols)),
                    device_id_type=MESH,
                )
    pl.semaphore_wait(barrier, rows * cols - 1)


def exchange_kernel(
    rows, cols, chunks,
    tensor_ref, pattern_ref, occ_ref, virt_ref, density_ref,
    out_ref,
    b_in, s_in, b_lines, wide_rows, part, landed, total, others,
    masked, virt_all, occ_all, moved, moved_cols, second,
    gather_send, gather_recv, spread_send, spread_recv,
    b_send, b_recv, m_send, m_recv, s_send, s_recv, own_sem, load_sem, row_send, row_recv, col_send, col_recv,
):
    me_row, me_col = lax.axis_index("row"), lax.axis_index("col")
    aux, local, orb = tensor_ref.shape
    strip = local // rows
    wide = orb // cols
    blocks = orb // BS
    quarter = virt_ref.shape[0] // cols
    row_steps = near_first(rows)

    def remote(src, dst, send, recv, to_row, to_col):
        copy = pltpu.make_async_remote_copy(
            src_ref=src, dst_ref=dst, send_sem=send, recv_sem=recv,
            device_id=(to_row, to_col), device_id_type=MESH,
        )
        copy.start()
        return copy

    load = pltpu.make_async_copy(tensor_ref, masked, load_sem)
    load.start()
    greet(me_row, me_col, rows, cols)

    share = pl.ds(pl.multiple_of(me_col * quarter, quarter), quarter)
    gathers = []
    owns = []
    for d, (src, dst) in enumerate(((virt_ref, virt_all), (occ_ref, occ_all))):
        own = pltpu.make_async_copy(src.at[share], dst.at[me_row, me_col], own_sem.at[d])
        own.start()
        owns.append(own)
        gathers.append([
            remote(src.at[share], dst.at[me_row, me_col],
                   gather_send.at[d, k], gather_recv.at[d, k],
                   partner(me_row, k, rows)[0], me_col)
            for k in row_steps
        ])

    block_row = (me_col * local) // BS

    def mask_one(p, carry):
        for j in range(blocks):
            keep = pattern_ref[block_row, j, p].astype(jnp.float32)
            piece = masked[p, :, j * BS:(j + 1) * BS].astype(jnp.float32)
            masked[p, :, j * BS:(j + 1) * BS] = (piece * keep).astype(jnp.bfloat16)
        return carry

    load.wait()
    lax.fori_loop(0, aux, mask_one, 0)

    b_copies = []
    for k in row_steps:
        to_row = partner(me_row, k, rows)[0]
        theirs = pl.ds(pl.multiple_of(to_row * strip, strip), strip)
        b_copies.append(remote(masked.at[:, theirs, :], b_in.at[me_row],
                               b_send.at[k], b_recv.at[k], to_row, me_col))
    own_part = pl.ds(pl.multiple_of(me_row * strip, strip), strip)
    own_b = pltpu.make_async_copy(masked.at[:, own_part, :], b_in.at[me_row], own_sem.at[2])
    own_b.start()

    spreads = []
    for d, full in enumerate((virt_all, occ_all)):
        owns[d].wait()
        for copy in gathers[d]:
            copy.wait_recv()
        spreads.append([
            remote(full.at[:, me_col], full.at[:, me_col],
                   spread_send.at[d, k], spread_recv.at[d, k],
                   me_row, partner(me_col, k, cols)[0])
            for k in range(1, cols)
        ])

    def take_density(full, d):
        for copy in spreads[d]:
            copy.wait()
        for copy in gathers[d]:
            copy.wait_send()
        values = full[...].reshape(orb, orb)
        lines = []
        for i in range(blocks):
            line = []
            for j in range(blocks):
                keep = density_ref[i, j].astype(jnp.float32)
                piece = values[i * BS:(i + 1) * BS, j * BS:(j + 1) * BS].astype(jnp.float32)
                line.append((piece * keep).astype(jnp.bfloat16))
            lines.append(jnp.concatenate(line, axis=1))
        full[...] = jnp.concatenate(lines, axis=0).reshape(full.shape)

    take_density(virt_all, 0)

    def move_one(p, carry):
        product = jnp.dot(masked[p], virt_all[...].reshape(orb, orb),
                          preferred_element_type=jnp.float32).astype(jnp.bfloat16)
        for j in range(cols):
            moved[j, p] = product[:, j * wide:(j + 1) * wide]
        return carry

    span = aux // chunks
    m_copies = []
    for h in range(chunks):
        lax.fori_loop(h * span, (h + 1) * span, move_one, 0)
        piece = pl.ds(h * span, span)
        copies = []
        for k in range(1, cols):
            to_col = partner(me_col, k, cols)[0]
            copies.append(remote(moved.at[to_col, piece], moved_cols.at[me_col, piece],
                                 m_send.at[h, k], m_recv.at[h, k], me_row, to_col))
        own = pltpu.make_async_copy(moved.at[me_col, piece], moved_cols.at[me_col, piece],
                                    own_sem.at[5 + h])
        own.start()
        m_copies.append(copies + [own])

    take_density(occ_all, 1)

    def second_two(p, carry):
        rhs = jnp.concatenate(
            [moved_cols[:, 2 * p + h].reshape(orb, wide) for h in range(2)], axis=1)
        product = jnp.dot(occ_all[...].reshape(orb, orb), rhs,
                          preferred_element_type=jnp.float32).astype(jnp.bfloat16)
        for h in range(2):
            second[2 * p + h] = product[:, h * wide:(h + 1) * wide]
        return carry

    lanes = pl.ds(pl.multiple_of(me_col * wide, wide), wide)

    def strip_of(to_row, to_col):
        return pl.ds(pl.multiple_of(to_col * local + to_row * strip, strip), strip)

    s_copies = [[] for _ in range(chunks)]
    for h in range(chunks):
        piece = pl.ds(h * span, span)
        for copy in m_copies[h]:
            copy.wait()
        lax.fori_loop(h * span // 2, (h + 1) * span // 2, second_two, 0)
        for k in [0] + row_steps:
            for q in range(cols):
                if k or q:
                    to_row, to_col = partner(me_row, k, rows)[0], partner(me_col, q, cols)[0]
                    s_copies[h].append(remote(
                        second.at[piece, strip_of(to_row, to_col), :],
                        s_in.at[me_row, piece, :, lanes],
                        s_send.at[h, k, q], s_recv.at[h, k, q], to_row, to_col))
    own_s = pltpu.make_async_copy(second.at[:, strip_of(me_row, me_col), :],
                                  s_in.at[me_row, :, :, lanes], own_sem.at[4])
    own_s.start()

    def widen(p, carry):
        rows_at = pl.ds(pl.multiple_of(p * aux * strip, aux * strip), aux * strip)
        for j in range(orb // BS):
            wide_rows[j, rows_at, :] = b_in[p, :, :, j * BS:(j + 1) * BS].reshape(
                aux * strip, BS).astype(jnp.float32)
        return carry

    def every(line, count):
        return jnp.concatenate(
            [wide_rows[j, pl.ds(line, count, stride=strip), :] for j in range(orb // BS)],
            axis=1).astype(jnp.bfloat16)

    own_b.wait()
    for copy in b_copies:
        copy.wait()
    lax.fori_loop(0, rows, widen, 0)
    for line in range(strip):
        b_lines[line] = every(line, rows * aux)

    own_s.wait()
    for h in range(chunks):
        for copy in s_copies[h]:
            copy.wait()
        count = rows * span
        for j in range(orb // BS):
            wide_rows[j, 0:count * strip, :] = s_in[
                :, h * span:(h + 1) * span, :, j * BS:(j + 1) * BS].reshape(
                count * strip, BS).astype(jnp.float32)
        chi = jnp.zeros((count, rows * aux), jnp.float32)
        for line in range(strip):
            chi = chi + lax.dot_general(every(line, count), b_lines[line], (((1,), (1,)), ((), ())),
                                        preferred_element_type=jnp.float32)
        part[:, h * span:(h + 1) * span, :] = chi.reshape(rows, span, rows * aux)

    copies = []
    for k in row_steps:
        to_row = partner(me_row, k, rows)[0]
        copies.append(remote(part.at[to_row], landed.at[k],
                             row_send.at[k], row_recv.at[k], to_row, me_col))
    value = part[me_row]
    for copy in copies:
        copy.wait()
    for k in range(1, rows):
        value = value + landed[k]
    total[...] = value
    copies = []
    for k in range(1, cols):
        to_col = partner(me_col, k, cols)[0]
        copies.append(remote(total, others.at[me_col],
                             col_send.at[k], col_recv.at[k], me_row, to_col))
    others[me_col] = value
    for copy in copies:
        copy.wait()
    value = others[0]
    for k in range(1, cols):
        value = value + others[k]
    out_ref[...] = value


def direct(rows, cols, three_centre, tensor_pattern, occ_density, virt_density, density_pattern):
    aux, local, orb = three_centre.shape
    strip, wide = local // rows, orb // cols
    quarter = occ_density.shape[0] // cols
    bf16 = jnp.bfloat16
    chunks = aux // 8
    total = rows * aux
    f32 = jnp.float32
    dma = pltpu.SemaphoreType.DMA
    vmem = pl.BlockSpec(memory_space=pltpu.VMEM)
    smem = pl.BlockSpec(memory_space=pltpu.SMEM)
    hbm = pl.BlockSpec(memory_space=pltpu.MemorySpace.HBM)
    return pl.pallas_call(
        functools.partial(exchange_kernel, rows, cols, chunks),
        out_shape=jax.ShapeDtypeStruct((aux, total), f32),
        in_specs=[hbm, smem, hbm, hbm, smem],
        out_specs=vmem,
        scratch_shapes=[
            pltpu.VMEM((rows, aux, strip, orb), bf16),
            pltpu.VMEM((rows, aux, strip, orb), bf16),
            pltpu.VMEM((strip, total, orb), bf16),
            pltpu.VMEM((orb // BS, total * strip, BS), f32),
            pltpu.VMEM((rows, aux, total), f32),
            pltpu.VMEM((rows, aux, total), f32),
            pltpu.VMEM((aux, total), f32),
            pltpu.VMEM((cols, aux, total), f32),
            pltpu.VMEM((aux, local, orb), bf16),
            pltpu.VMEM((rows, cols, quarter, orb), bf16),
            pltpu.VMEM((rows, cols, quarter, orb), bf16),
            pltpu.VMEM((cols, aux, local, wide), bf16),
            pltpu.VMEM((cols, aux, local, wide), bf16),
            pltpu.VMEM((aux, orb, wide), bf16),
            dma((2, rows)), dma((2, rows)), dma((2, cols)), dma((2, cols)),
            dma((rows,)), dma((rows,)), dma((chunks, cols)), dma((chunks, cols)),
            dma((chunks, rows, cols)), dma((chunks, rows, cols)), dma((5 + chunks,)), dma(()),
            dma((rows,)), dma((rows,)), dma((cols,)), dma((cols,)),
        ],
        compiler_params=pltpu.CompilerParams(
            collective_id=0, has_side_effects=True, vmem_limit_bytes=67_000_000),
    )(three_centre, tensor_pattern.transpose(1, 2, 0), occ_density, virt_density,
      density_pattern)


def staged(three_centre, tensor_pattern, occ_density, virt_density, density_pattern):
    aux_count = three_centre.shape[0]
    local_rows = three_centre.shape[1]
    orbital_count = three_centre.shape[2]
    offset = lax.axis_index("col") * local_rows
    row_blocks = (offset + jnp.arange(local_rows, dtype=jnp.int32)) // BS
    pattern_rows = jnp.take(tensor_pattern, row_blocks, axis=1)
    tensor_mask = jnp.repeat(pattern_rows, BS, 2).astype(jnp.bfloat16)
    masked = three_centre * tensor_mask
    occupied_full, virtual_full = (
        lax.all_gather(occ_density, "row", axis=0, tiled=True),
        lax.all_gather(virt_density, "row", axis=0, tiled=True),
    )
    density_mask = expand_blocks(density_pattern, BS, 0, 1).astype(jnp.bfloat16)
    occupied = occupied_full * density_mask
    virtual = virtual_full * density_mask
    moved = jnp.dot(
        masked.reshape(aux_count * local_rows, orbital_count),
        virtual,
        preferred_element_type=jnp.float32,
    ).astype(jnp.bfloat16)
    moved = moved.reshape(aux_count, local_rows, orbital_count)
    moved_cols, regrouped = (
        lax.all_to_all(moved, "col", split_axis=2, concat_axis=1, tiled=True),
        lax.all_to_all(masked, "col", split_axis=2, concat_axis=1, tiled=True),
    )
    second = jnp.einsum(
        "lm,pms->pls", occupied, moved_cols, preferred_element_type=jnp.float32
    ).astype(jnp.bfloat16)
    grouped_left, grouped_right = (
        lax.all_to_all(second, "row", split_axis=1, concat_axis=0, tiled=True),
        lax.all_to_all(regrouped, "row", split_axis=1, concat_axis=0, tiled=True),
    )
    total_aux = grouped_left.shape[0]
    left_flat = grouped_left.reshape(total_aux, -1)
    right_flat = grouped_right.reshape(total_aux, -1)
    partial_chi = lax.dot_general(
        left_flat, right_flat, (((1,), (1,)), ((), ())), preferred_element_type=jnp.float32
    )
    row_summed = lax.psum_scatter(partial_chi, "row", scatter_dimension=0, tiled=True)
    return lax.psum(row_summed, "col")


def solution(mesh):
    rows, cols = mesh.shape["row"], mesh.shape["col"]

    def per_device(three_centre, tensor_pattern, occ_density, virt_density, density_pattern):
        aux, local, orb = three_centre.shape
        aligned = (
            local % (16 * rows) == 0 and occ_density.shape[0] % (16 * cols) == 0
            and orb % (128 * cols) == 0 and BS % local == 0 and aux % 8 == 0
        )
        args = (three_centre, tensor_pattern, occ_density, virt_density, density_pattern)
        return direct(rows, cols, *args) if aligned else staged(*args)

    in_specs = (P("row", "col", None), P("row", None, None), P("row", None), P("row", None), P())
    out_specs = P("row", None)
    return jax.shard_map(
        per_device, mesh=mesh, in_specs=in_specs, out_specs=out_specs, check_vma=False
    )
```
